256 devices in a mesh: dp: 8 (over z), expert: 32 (over y, x, core).
Axes of the slice: x: 4, y: 4, z: 8, core: 2. Of those that a mesh axis runs over, the one named last changes fastest.
Arguments:
- activations: bfloat16 [131072, 1024], P(('dp', 'expert')), may hold values from -6 to 6
- out_grad: bfloat16 [131072, 1024], P(('dp', 'expert')), may hold values from -1.5 to 1.5
- w_in: bfloat16 [1024, 64, 1024], P('dp', 'expert'), may hold values from -0.1875 to 0.1875
- w_out: bfloat16 [1024, 64, 1024], P('dp', 'expert'), may hold values from -0.1875 to 0.1875
- token_lists: int32 [8, 64, 512], P('dp', 'expert'), may hold values from 0 to 16383, as said below
- valid_mask: int32 [8, 64, 512], P('dp', 'expert'), may hold values from 0 to 1, as said below
- gate_weights: float32 [8, 64, 512], P('dp', 'expert'), may hold values from 0.05 to 1
Outputs:
- token_grad: bfloat16 [131072, 1024], P(('dp', 'expert'))
- gate_grad: float32 [8, 64, 512], P('dp', 'expert')
- w_in_grad: bfloat16 [1024, 64, 1024], P('dp', 'expert')
- w_out_grad: bfloat16 [1024, 64, 1024], P('dp', 'expert')
The draws below stay inside these ranges and needn't reach their ends.
Inputs may be any that keep to these rules, and one draw needn't show every extreme that they name: `token_lists`: entries are token numbers within the data group (its 16384 tokens in the order of the expert axis). Valid entries of one list are distinct; padded entries are 0. Among the valid entries of the 2 lists of one index of the expert axis, at most 48 lie in the 512 tokens of any one index of that axis; in every group some index of the expert axis holds exactly 48 tokens chosen by the lists of every index. `valid_mask`: each list's ones form a prefix of 256 or more entries; some list of every group is full.
All inputs are finite; a program needn't handle non-finite values.
Results may differ from the reference program's by a relative error of at most 0.017.
Values may be sent and summed in bfloat16 or wider, within the bound.
A program may use at most 128 MiB of HBM per device.

```python
import math
import jax
import jax.numpy as jnp
from jax import lax

D = 1024
F = 1024
EXP_DEV = 2
TOK_DEV = 512
EXPERTS = 64
GROUP_TOK = 16384
TOKENS = 131072
CAP = 512
MOST = 48
N_DP = 8
N_EXPERT = 32


def pick_tables(key):
    base = jax.random.fold_in(key, 4242)
    key_perm, key_forced, key_local, key_count, key_full = jax.random.split(base, 5)
    tickets = N_EXPERT * MOST
    picks = EXP_DEV * CAP
    perm_keys = jax.random.split(key_perm, N_DP * N_EXPERT)
    shuffled = jax.vmap(lambda single: jax.random.permutation(single, tickets))(perm_keys).reshape(N_DP, N_EXPERT, tickets).astype(jnp.int32)
    forced = jax.random.randint(key_forced, (N_DP, 1, 1), 0, N_EXPERT)
    priority = jnp.where(shuffled // MOST == forced, 0, tickets) + jnp.arange(tickets, dtype=jnp.int32)[None, None, :]
    order = jnp.argsort(priority, axis=-1)
    chosen = jnp.take_along_axis(shuffled, order, axis=-1)[:, :, :picks]
    owners = chosen // MOST
    local_keys = jax.random.split(key_local, N_DP * N_EXPERT * N_EXPERT)
    local_perm = jax.vmap(lambda single: jax.random.permutation(single, TOK_DEV)[:MOST])(local_keys).reshape(N_DP, N_EXPERT, tickets).astype(jnp.int32)
    local_rows = jnp.take_along_axis(local_perm, chosen, axis=-1)
    lists = (owners * TOK_DEV + local_rows).reshape(N_DP, EXPERTS, CAP)
    counts = jax.random.randint(key_count, (N_DP, EXPERTS), CAP // 2, CAP + 1)
    full_list = jax.random.randint(key_full, (N_DP, 1), 0, EXPERTS)
    counts = jnp.where(jnp.arange(EXPERTS, dtype=jnp.int32)[None, :] == full_list, CAP, counts)
    valid = (jnp.arange(CAP, dtype=jnp.int32)[None, None, :] < counts[:, :, None]).astype(jnp.int32)
    lists = jnp.where(valid == 1, lists, 0).astype(jnp.int32)
    return (lists, valid)


def draw_token_lists(key, part):
    return pick_tables(key)[0]


def draw_valid_mask(key, part):
    return pick_tables(key)[1]


def level_of(rng, shape, shards, smallest, high):
    def one(axis_at, blocks):
        steps = jax.random.uniform(jax.random.fold_in(jax.random.fold_in(rng, 6), axis_at), (blocks,), jnp.float32, smallest / len(shards), high / len(shards))
        return jnp.repeat(jnp.exp(steps), shape[axis_at] // blocks).reshape((-1,) + (1,) * (len(shape) - axis_at - 1))

    factor_of = one(*shards[0])
    for cut in shards[1:]:
        factor_of = factor_of * one(*cut)
    return factor_of


def bell_draw(own_key, dims, scale, limit, shards=(), kind=jnp.bfloat16):
    values = scale * jax.random.normal(own_key, dims, jnp.float32)
    if shards:
        values = values * level_of(own_key, dims, shards, -0.22, 0.18)
    return jnp.clip(values, -limit, limit).astype(kind)


def setup_inputs(seed: int = 0) -> dict:
    arg_keys = jax.random.split(jax.random.key(seed), 8)
    activations = bell_draw(arg_keys[0], (TOKENS, D), 1.0, 6.0, ((0, 256),))
    out_grad = bell_draw(arg_keys[1], (TOKENS, D), 0.25, 1.5, ((0, 256),))
    w_in = bell_draw(arg_keys[2], (D, EXPERTS, F), D ** -0.5, 0.1875, ((0, 8), (1, 32)))
    w_out = bell_draw(arg_keys[3], (F, EXPERTS, D), F ** -0.5, 0.1875, ((0, 8), (1, 32)))
    token_lists = draw_token_lists(jax.random.fold_in(arg_keys[7], 71), 0)
    valid_mask = draw_valid_mask(jax.random.fold_in(arg_keys[7], 71), 0)
    gate_weights = jnp.clip(jnp.exp(math.log(1.0) - 2.9957323 * jax.random.uniform(arg_keys[6], (N_DP, EXPERTS, CAP), jnp.float32) ** level_of(arg_keys[6], (N_DP, EXPERTS, CAP), ((0, 8), (1, 32)), -0.2, 0.2)), 0.05, 1.0)
    return dict(activations=activations, out_grad=out_grad, w_in=w_in, w_out=w_out, token_lists=token_lists, valid_mask=valid_mask, gate_weights=gate_weights)


gelu_coef = 0.7978845608028654
cubic_coef = 0.044715


def gelu_parts(value):
    inner = gelu_coef * (value + cubic_coef * value * value * value)
    tangent = jnp.tanh(inner)
    result = 0.5 * value * (1.0 + tangent)
    slope = 0.5 * (1.0 + tangent) + 0.5 * value * (1.0 - tangent * tangent) * gelu_coef * (1.0 + 3.0 * cubic_coef * value * value)
    return result, slope


def reference(activations, out_grad, w_in, w_out, token_lists, valid_mask, gate_weights):
    hp = lax.Precision.HIGHEST
    group_x = activations.reshape(N_DP, GROUP_TOK, D)
    group_g = out_grad.reshape(N_DP, GROUP_TOK, D)
    in_wide = w_in.astype(jnp.float32)
    out_wide = w_out.astype(jnp.float32)

    def one_group(totals, inputs):
        x_rows, g_rows, lists, valid, gates = inputs
        live = (valid == 1)[:, :, None]
        picked_in = jnp.where(live, x_rows[lists], jnp.zeros((), jnp.bfloat16))
        picked_grad = jnp.where(live, g_rows[lists], jnp.zeros((), jnp.bfloat16))
        pre_act = jnp.einsum("ecd,def->ecf", picked_in.astype(jnp.float32), in_wide, precision=hp)
        hidden, slope = gelu_parts(pre_act)
        hidden = hidden.astype(jnp.bfloat16)
        expert_out = jnp.einsum("ecf,fed->ecd", hidden.astype(jnp.float32), out_wide, precision=hp)
        gate_grad = jnp.sum(picked_grad.astype(jnp.float32) * expert_out, axis=-1)
        scaled = ((gates * valid.astype(jnp.float32))[:, :, None] * picked_grad.astype(jnp.float32)).astype(jnp.bfloat16)
        hidden_grad = jnp.einsum("ecd,fed->ecf", scaled.astype(jnp.float32), out_wide, precision=hp)
        pre_grad = (hidden_grad * slope).astype(jnp.bfloat16)
        in_grad = jnp.einsum("ecf,def->ecd", pre_grad.astype(jnp.float32), in_wide, precision=hp).astype(jnp.bfloat16)
        token_grad = jax.ops.segment_sum(in_grad.reshape(-1, D).astype(jnp.float32), lists.reshape(-1).astype(jnp.int32), num_segments=GROUP_TOK).astype(jnp.bfloat16)
        in_part = jnp.einsum("ecd,ecf->def", picked_in.astype(jnp.float32), pre_grad.astype(jnp.float32), precision=hp).astype(jnp.bfloat16)
        out_part = jnp.einsum("ecf,ecd->fed", hidden.astype(jnp.float32), scaled.astype(jnp.float32), precision=hp).astype(jnp.bfloat16)
        updated = (totals[0] + in_part.astype(jnp.float32), totals[1] + out_part.astype(jnp.float32))
        return updated, (token_grad, gate_grad)

    start = (jnp.zeros((D, EXPERTS, F), jnp.float32), jnp.zeros((F, EXPERTS, D), jnp.float32))
    sums, per_group = lax.scan(one_group, start, (group_x, group_g, token_lists, valid_mask, gate_weights))
    token_grad = per_group[0].reshape(TOKENS, D)
    return token_grad, per_group[1], sums[0].astype(jnp.bfloat16), sums[1].astype(jnp.bfloat16)
```

```python
import jax
import jax.numpy as jnp
from jax import lax
from jax.sharding import PartitionSpec as P

gelu_coef = 0.7978845608028654
cubic_coef = 0.044715
bf16 = jnp.bfloat16
f32 = jnp.float32


def gelu_parts(value):
    inner = gelu_coef * (value + cubic_coef * value * value * value)
    tangent = jnp.tanh(inner)
    result = 0.5 * value * (1.0 + tangent)
    slope = 0.5 * (1.0 + tangent) + 0.5 * value * (1.0 - tangent * tangent) * gelu_coef * (
        1.0 + 3.0 * cubic_coef * value * value
    )
    return (result, slope)


def dot(a, b, ca, cb):
    return lax.dot_general(a, b, (((ca,), (cb,)), ((), ())), preferred_element_type=f32)


def on_device(activations, out_grad, w_in, w_out, token_lists, valid_mask, gate_weights):
    n_peers = lax.axis_size("expert")
    tok_local, width = activations.shape
    _, exp_local, cap_len = token_lists.shape
    shard, _, hid = w_in.shape
    picks = exp_local * cap_len
    slots = max(2, 3 * picks // (2 * n_peers))
    n_slots = n_peers * slots

    w_in_rows = w_in.reshape(shard, exp_local * hid)
    w_out_rows = w_out.reshape(w_out.shape[0], exp_local * width)
    full_in = lax.all_gather(w_in_rows, "dp", axis=0, tiled=True)
    full_out = lax.all_gather(w_out_rows, "dp", axis=0, tiled=True)

    flat = token_lists.reshape(picks)
    live = valid_mask.reshape(picks) == 1
    owners = jnp.where(live, flat // tok_local, -1)
    local = flat % tok_local
    peers = jnp.arange(n_peers, dtype=jnp.int32)
    hits = (owners[:, None] == peers[None, :]).astype(bf16)
    order = jnp.arange(picks, dtype=jnp.int32)
    earlier = (order[None, :] < order[:, None]).astype(bf16)
    rank_all = dot(earlier, hits, 1, 0)
    before = jnp.sum(rank_all * hits.astype(f32), axis=1).astype(jnp.int32)
    slot_of = jnp.where(live, owners * slots + before, -1)
    place = (before[:, None] == jnp.arange(slots, dtype=jnp.int32)[None, :]).astype(bf16)
    high = (local // 32 + 1).astype(bf16)[:, None]
    low = (local % 32).astype(bf16)[:, None]
    both = jnp.concatenate([hits * high, hits * low], axis=1)
    coded = dot(both, place, 0, 0).astype(jnp.int32)
    table = coded[:n_peers] * 32 + coded[n_peers:] - 32

    wanted = lax.all_to_all(table, "expert", split_axis=0, concat_axis=0, tiled=True)
    wanted = wanted.reshape(n_slots)
    toks = jnp.arange(tok_local, dtype=jnp.int32)
    send = (wanted[:, None] == toks[None, :]).astype(bf16)
    out_x = dot(send, activations, 1, 0).astype(bf16)
    out_g = dot(send, out_grad, 1, 0).astype(bf16)
    got_x = lax.all_to_all(out_x, "expert", split_axis=0, concat_axis=0, tiled=True)
    got_g = lax.all_to_all(out_g, "expert", split_axis=0, concat_axis=0, tiled=True)

    pick = (slot_of[:, None] == jnp.arange(n_slots, dtype=jnp.int32)[None, :]).astype(bf16)
    picked_in = dot(pick, got_x, 1, 0).astype(bf16)
    gates = (gate_weights * valid_mask.astype(f32)).reshape(picks)

    ins, outs, grads, gate_parts = [], [], [], []
    hiddens, slopes = [], []
    for e in range(exp_local):
        rows = slice(e * cap_len, (e + 1) * cap_len)
        hidden, slope = gelu_parts(dot(picked_in[rows], full_in[:, e * hid : (e + 1) * hid], 1, 0))
        hiddens.append(hidden.astype(bf16))
        slopes.append(slope)
    picked_grad = dot(pick, got_g, 1, 0).astype(bf16)
    scaled_all = (gates[:, None] * picked_grad.astype(f32)).astype(bf16)
    pre_grads = []
    for e in range(exp_local):
        rows = slice(e * cap_len, (e + 1) * cap_len)
        outs.append(dot(hiddens[e], scaled_all[rows], 0, 0).astype(bf16))
    w_out_grad = lax.psum_scatter(
        jnp.concatenate(outs, axis=1), "dp", scatter_dimension=0, tiled=True
    )
    for e in range(exp_local):
        rows = slice(e * cap_len, (e + 1) * cap_len)
        w_o = full_out[:, e * width : (e + 1) * width]
        pre_grad = (dot(scaled_all[rows], w_o, 1, 1) * slopes[e]).astype(bf16)
        pre_grads.append(pre_grad)
        ins.append(dot(picked_in[rows], pre_grad, 0, 0).astype(bf16))
    w_in_grad = lax.psum_scatter(
        jnp.concatenate(ins, axis=1), "dp", scatter_dimension=0, tiled=True
    )
    for e in range(exp_local):
        rows = slice(e * cap_len, (e + 1) * cap_len)
        grads.append(dot(pre_grads[e], full_in[:, e * hid : (e + 1) * hid], 1, 1).astype(bf16))
        expert_out = dot(hiddens[e], full_out[:, e * width : (e + 1) * width], 1, 0)
        gate_parts.append(jnp.sum(picked_grad[rows].astype(f32) * expert_out, axis=-1))
    in_grad = jnp.concatenate(grads, axis=0)
    back = dot(pick, in_grad, 0, 0).astype(bf16)
    returned = lax.all_to_all(back, "expert", split_axis=0, concat_axis=0, tiled=True)
    token_grad = dot(send, returned, 0, 0).astype(bf16)
    return (
        token_grad,
        jnp.stack(gate_parts)[None],
        w_in_grad.reshape(shard, exp_local, hid),
        w_out_grad.reshape(w_out.shape[0], exp_local, width),
    )


def solution(mesh):
    tokens = P(("dp", "expert"), None)
    split = P("dp", "expert", None)
    return jax.shard_map(
        on_device,
        mesh=mesh,
        in_specs=(tokens, tokens, split, split, split, split, split),
        out_specs=(tokens, split, split, split),
        check_vma=False,
    )
```

```python
import functools
import jax
import jax.numpy as jnp
from jax import lax
from jax.experimental import pallas as pl
from jax.experimental.pallas import tpu as pltpu
from jax.sharding import PartitionSpec as P

gelu_coef = 0.7978845608028654
cubic_coef = 0.044715
bf16 = jnp.bfloat16
f32 = jnp.float32
i32 = jnp.int32
VMEM_BYTES = 67043328


def gelu_parts(value):
    inner = gelu_coef * (value + cubic_coef * value * value * value)
    tangent = jnp.tanh(inner)
    result = 0.5 * value * (1.0 + tangent)
    slope = 0.5 * (1.0 + tangent) + 0.5 * value * (1.0 - tangent * tangent) * gelu_coef * (
        1.0 + 3.0 * cubic_coef * value * value
    )
    return (result, slope)


def dot(a, b, ca, cb):
    return lax.dot_general(a, b, (((ca,), (cb,)), ((), ())), preferred_element_type=f32)


def loop(count, body):
    def step(i, carry):
        body(i)
        return carry

    lax.fori_loop(0, count, step, 0)


def layer_kernel(
    n_peers, n_ring, slots, group, tile,
    x_ref, g_ref, wi_ref, wo_ref, table_ref, slot_col, slot_row, gate_col,
    tok_ref, gate_ref, wig_ref, wog_ref,
    full, send_x, send_g, recv_x, recv_g, recv_b, sel, want,
    picked_x, picked_g, scaled, hidden, slope, pre_grad, in_grad, ring,
    ag_send, ag_recv, rs_send, rs_recv, t_send, t_recv, a_send, a_recv, own_sem,
):
    me = lax.axis_index("expert")
    z = lax.axis_index("dp")
    tokens, width = x_ref.shape
    shard = wi_ref.shape[1]
    picks = slot_col.shape[0]
    cap = picks // 2
    n_slots = n_peers * slots
    span = group * slots
    half = n_ring // 2
    tiles = picks // tile
    per_expert = cap // tile

    def rows_of(i):
        return pl.ds(pl.multiple_of(i * tile, tile), tile)

    def expert_rows(e):
        return pl.ds(pl.multiple_of(e * cap, cap), cap)

    def peer_rows(p):
        return pl.ds(pl.multiple_of(p * slots, slots), slots)

    def shard_rows(s):
        return pl.ds(pl.multiple_of(s * shard, shard), shard)

    barrier = pltpu.get_barrier_semaphore()

    def greet(i):
        pl.semaphore_signal(
            barrier, inc=1, device_id={"expert": lax.rem(me + i + 1, n_peers)},
            device_id_type=pl.DeviceIdType.MESH,
        )

    loop(n_peers - 1, greet)
    for step in (1, n_ring - 1):
        pl.semaphore_signal(
            barrier, inc=1, device_id={"dp": lax.rem(z + step, n_ring)},
            device_id_type=pl.DeviceIdType.MESH,
        )
    pl.semaphore_wait(barrier, n_peers + 1)

    def neighbour(d):
        return lax.rem(z + 1 + d * (n_ring - 2), n_ring)

    def ag_copy(m, e, d, s, own):
        holder = lax.rem(z + n_ring - s + d * (2 * s), n_ring)
        place = full.at[m, e, shard_rows(holder), :]
        source = (wi_ref, wo_ref)[m].at[e] if own else place
        return pltpu.make_async_remote_copy(
            src_ref=source, dst_ref=place,
            send_sem=ag_send.at[m, e, d, s], recv_sem=ag_recv.at[m, e, d, s],
            device_id={"dp": neighbour(d)}, device_id_type=pl.DeviceIdType.MESH,
        )

    def ag_step(m, s):
        def one(j):
            e, d = j // 2, j % 2
            if s > 0:
                ag_copy(m, e, d, s - 1, False).wait_recv()
            if s < half:
                ag_copy(m, e, d, s, s == 0).start()

        def last(j):
            if s > 0:
                ag_copy(m, j, j, s - 1, False).wait_recv()
            if s < half:
                ag_copy(m, j, j, s, s == 0).start()

        def tail(e):
            ag_copy(m, e, 1 - e, s - 1, False).wait_recv()

        if s < half - 1:
            loop(4, one)
        else:
            loop(2, last)
            if s == half - 1 and s > 0:
                loop(2, tail)

    def own_copy(m, e):
        return pltpu.make_async_copy(
            (wi_ref, wo_ref)[m].at[e], full.at[m, e, shard_rows(z), :], own_sem.at[m, e]
        )

    ag_step(0, 0)
    ag_step(1, 0)

    def table_copy(q):
        return pltpu.make_async_remote_copy(
            src_ref=table_ref.at[q], dst_ref=want.at[me],
            send_sem=t_send.at[q], recv_sem=t_recv.at[me],
            device_id={"expert": q}, device_id_type=pl.DeviceIdType.MESH,
        )

    def table_arrival(p):
        return pltpu.make_async_remote_copy(
            src_ref=table_ref.at[p], dst_ref=want.at[p],
            send_sem=t_send.at[p], recv_sem=t_recv.at[p],
            device_id={"expert": p}, device_id_type=pl.DeviceIdType.MESH,
        )

    def other(i):
        return lax.rem(me + lax.rem((i + 1) * 13, n_peers), n_peers)

    loop(n_peers - 1, lambda i: table_copy(other(i)).start())
    for m in range(2):
        for e in range(2):
            own_copy(m, e).start()
    mine = pltpu.make_async_copy(table_ref.at[me], want.at[me], own_sem.at[2, 0])
    mine.start()
    mine.wait()
    loop(n_peers - 1, lambda i: table_arrival(other(i)).wait_recv())

    for k in range(n_peers // group):
        asked = jnp.sum(want[k * group : (k + 1) * group], axis=0)
        token = lax.broadcasted_iota(i32, (tokens, span), 0) + 1
        sel[:, k * span : (k + 1) * span] = jnp.where(token == asked, 1.0, 0.0).astype(bf16)

    def gather(source, target):
        for k in range(n_peers // group):
            rows = slice(k * span, (k + 1) * span)
            target[rows, :] = dot(sel[:, rows], source[...], 0, 0).astype(bf16)

    def row_copy(phase, source, target, q):
        return pltpu.make_async_remote_copy(
            src_ref=source.at[peer_rows(q), :], dst_ref=target.at[peer_rows(me), :],
            send_sem=a_send.at[phase, q], recv_sem=a_recv.at[phase, me],
            device_id={"expert": q}, device_id_type=pl.DeviceIdType.MESH,
        )

    def row_arrival(phase, source, target, p):
        return pltpu.make_async_remote_copy(
            src_ref=source.at[peer_rows(p), :], dst_ref=target.at[peer_rows(p), :],
            send_sem=a_send.at[phase, p], recv_sem=a_recv.at[phase, p],
            device_id={"expert": p}, device_id_type=pl.DeviceIdType.MESH,
        )

    def own_rows(phase, source, target):
        return pltpu.make_async_copy(
            source.at[peer_rows(me), :], target.at[peer_rows(me), :], own_sem.at[3, phase]
        )

    def send_all(phase, source, target):
        loop(n_peers - 1, lambda i: row_copy(phase, source, target, other(i)).start())
        own_rows(phase, source, target).start()

    def receive_all(phase, source, target):
        own_rows(phase, source, target).wait()
        loop(n_peers - 1, lambda i: row_arrival(phase, source, target, other(i)).wait_recv())

    def sent_all(phase, source, target):
        loop(n_peers - 1, lambda i: row_copy(phase, source, target, other(i)).wait_send())

    gather(x_ref, send_x)
    send_all(0, send_x, recv_x)
    if half > 1:
        ag_step(0, 1)
    gather(g_ref, send_g)
    send_all(1, send_g, recv_g)
    for s in range(2, half):
        ag_step(0, s)
    if half > 1:
        ag_step(1, 1)
    ag_step(0, half)
    for e in range(2):
        own_copy(0, e).wait()
    receive_all(0, send_x, recv_x)

    def pick_tile(i):
        at = lax.broadcasted_iota(i32, (tile, n_slots), 1)
        return jnp.where(slot_col[rows_of(i), :] == at, 1.0, 0.0).astype(bf16)

    def forward(i):
        rows = rows_of(i)
        picked = dot(pick_tile(i), recv_x[...], 1, 0).astype(bf16)
        picked_x[rows, :] = picked
        value, grade = gelu_parts(dot(picked, full[0, i // per_expert], 1, 0))
        hidden[rows, :] = value.astype(bf16)
        slope[rows, :] = grade

    loop(tiles, forward)
    for s in range(2, half + 1):
        ag_step(1, s)
    if half == 1:
        ag_step(1, 1)
    for e in range(2):
        own_copy(1, e).wait()
    receive_all(1, send_g, recv_g)

    def arrive_grad(i):
        rows = rows_of(i)
        grad = dot(pick_tile(i), recv_g[...], 1, 0).astype(bf16)
        picked_g[rows, :] = grad
        scaled[rows, :] = (gate_col[rows, :] * grad.astype(f32)).astype(bf16)

    loop(tiles, arrive_grad)

    def part(m, e, t):
        columns = pl.ds(pl.multiple_of(t * shard, shard), shard)
        left, right = ((picked_x, pre_grad), (hidden, scaled))[m]
        return dot(left[expert_rows(e), columns], right[expert_rows(e), :], 0, 0)

    def rs_copy(m, e, d, s):
        return pltpu.make_async_remote_copy(
            src_ref=ring.at[m, e, d, s], dst_ref=ring.at[m, e, d, s + 1],
            send_sem=rs_send.at[m, e, d, s], recv_sem=rs_recv.at[m, e, d, s],
            device_id={"dp": neighbour(d)}, device_id_type=pl.DeviceIdType.MESH,
        )

    def rs_hop(m, e, d, s, hops):
        far = hops - s
        block = part(m, e, lax.rem(z + n_ring + far - 2 * d * far, n_ring))
        if s > 0:
            rs_copy(m, e, d, s - 1).wait_recv()
            block = block + ring[m, e, d, s].astype(f32)
        ring[m, e, d, s] = block.astype(bf16)
        rs_copy(m, e, d, s).start()

    def rs_step(m, s):
        loop(2, lambda e: rs_hop(m, e, e, s, half))
        if s < half - 1:
            loop(2, lambda e: rs_hop(m, e, 1 - e, s, half - 1))

    def rs_final(m, target):
        def one(e):
            total = part(m, e, z)
            rs_copy(m, e, e, half - 1).wait_recv()
            total = total + ring[m, e, e, half].astype(f32)
            if half > 1:
                rs_copy(m, e, 1 - e, half - 2).wait_recv()
                total = total + ring[m, e, 1 - e, half - 1].astype(f32)
            target[e] = total.astype(bf16)

        loop(2, one)

    def backward(i):
        rows = rows_of(i)
        wide = dot(scaled[rows, :], full[1, i // per_expert], 1, 1)
        pre_grad[rows, :] = (wide * slope[rows, :]).astype(bf16)

    def to_input(i):
        rows = rows_of(i)
        in_grad[rows, :] = dot(pre_grad[rows, :], full[0, i // per_expert], 1, 1).astype(bf16)

    def back(k):
        at = lax.broadcasted_iota(i32, (span, picks), 0) + k * span
        place = jnp.where(slot_row[...] == at, 1.0, 0.0).astype(bf16)
        rows = pl.ds(pl.multiple_of(k * span, span), span)
        send_x[rows, :] = dot(place, in_grad[...], 1, 0).astype(bf16)

    def gate_part(i):
        rows = rows_of(i)
        wide = dot(hidden[rows, :], full[1, i // per_expert], 1, 0)
        gate_ref[rows, :] = jnp.sum(picked_g[rows, :].astype(f32) * wide, axis=1, keepdims=True)

    rs_step(1, 0)
    loop(tiles, backward)
    rs_step(0, 0)
    loop(tiles, to_input)
    sent_all(0, send_x, recv_x)
    loop(n_peers // group, back)
    send_all(2, send_x, recv_b)
    if half > 1:
        rs_step(1, 1)
        rs_step(0, 1)
    loop(tiles, gate_part)
    for s in range(2, half):
        rs_step(1, s)
        rs_step(0, s)
    receive_all(2, send_x, recv_b)
    tok_ref[...] = dot(sel[...], recv_b[...], 1, 0).astype(bf16)
    rs_final(1, wog_ref)
    rs_final(0, wig_ref)

    loop(n_peers - 1, lambda i: table_copy(other(i)).wait_send())
    sent_all(1, send_g, recv_g)
    sent_all(2, send_x, recv_b)
    for m in range(2):
        for s in range(half):
            for e in range(2):
                for d in range(2):
                    if s < half - 1 or e == d:
                        ag_copy(m, e, d, s, s == 0).wait_send()
                        rs_copy(m, e, d, s).wait_send()


def on_device(activations, out_grad, w_in, w_out, token_lists, valid_mask, gate_weights):
    n_peers = lax.axis_size("expert")
    n_ring = lax.axis_size("dp")
    me = lax.axis_index("expert")
    tok_local, width = activations.shape
    _, exp_local, cap_len = token_lists.shape
    shard, _, hid = w_in.shape
    picks = exp_local * cap_len
    slots = max(2, 3 * picks // (2 * n_peers))
    n_slots = n_peers * slots
    group = min(8, n_peers)
    tile = min(256, cap_len)

    flat = token_lists.reshape(picks)
    live = valid_mask.reshape(picks) == 1
    owners = jnp.where(live, flat // tok_local, -1)
    local = flat % tok_local
    peers = jnp.arange(n_peers, dtype=i32)
    hits = (owners[:, None] == peers[None, :]).astype(bf16)
    order = jnp.arange(picks, dtype=i32)
    earlier = (order[None, :] < order[:, None]).astype(bf16)
    rank_all = dot(earlier, hits, 1, 0)
    before = jnp.sum(rank_all * hits.astype(f32), axis=1).astype(i32)
    slot_of = jnp.where(live, owners * slots + before, -1)
    lane = before + (me % group) * slots
    place = (lane[:, None] == jnp.arange(group * slots, dtype=i32)[None, :]).astype(bf16)
    high = (local // 32).astype(bf16)[:, None]
    low = (local % 32 + 1).astype(bf16)[:, None]
    both = jnp.concatenate([hits * high, hits * low], axis=1)
    coded = dot(both, place, 0, 0).astype(i32)
    table = coded[:n_peers] * 32 + coded[n_peers:]
    gates = (gate_weights * valid_mask.astype(f32)).reshape(picks, 1)

    vmem = pl.BlockSpec(memory_space=pltpu.VMEM)
    dma = pltpu.SemaphoreType.DMA
    rows = (n_slots, width)
    half = n_ring // 2
    token_grad, gate_grad, w_in_grad, w_out_grad = pl.pallas_call(
        functools.partial(layer_kernel, n_peers, n_ring, slots, group, tile),
        out_shape=(
            jax.ShapeDtypeStruct((tok_local, width), bf16),
            jax.ShapeDtypeStruct((picks, 1), f32),
            jax.ShapeDtypeStruct((exp_local, shard, hid), bf16),
            jax.ShapeDtypeStruct((exp_local, shard, width), bf16),
        ),
        in_specs=[vmem] * 8,
        out_specs=(vmem,) * 4,
        scratch_shapes=[
            pltpu.VMEM((2, exp_local, width, hid), bf16),
            pltpu.VMEM(rows, bf16),
            pltpu.VMEM(rows, bf16),
            pltpu.VMEM(rows, bf16),
            pltpu.VMEM(rows, bf16),
            pltpu.VMEM(rows, bf16),
            pltpu.VMEM((tok_local, n_slots), bf16),
            pltpu.VMEM((n_peers, 1, group * slots), i32),
            pltpu.VMEM((picks, width), bf16),
            pltpu.VMEM((picks, width), bf16),
            pltpu.VMEM((picks, width), bf16),
            pltpu.VMEM((picks, hid), bf16),
            pltpu.VMEM((picks, hid), f32),
            pltpu.VMEM((picks, hid), bf16),
            pltpu.VMEM((picks, width), bf16),
            pltpu.VMEM((2, exp_local, 2, half + 1, shard, width), bf16),
            dma((2, 2, 2, half)),
            dma((2, 2, 2, half)),
            dma((2, 2, 2, half)),
            dma((2, 2, 2, half)),
            dma((n_peers,)),
            dma((n_peers,)),
            dma((3, n_peers)),
            dma((3, n_peers)),
            dma((4, 3)),
        ],
        compiler_params=pltpu.CompilerParams(
            collective_id=0, has_side_effects=True, vmem_limit_bytes=VMEM_BYTES
        ),
    )(
        activations,
        out_grad,
        w_in.transpose(1, 0, 2),
        w_out.transpose(1, 0, 2),
        table.reshape(n_peers, 1, group * slots),
        slot_of.reshape(picks, 1),
        slot_of.reshape(1, picks),
        gates,
    )
    return (
        token_grad,
        gate_grad.reshape(1, exp_local, cap_len),
        w_in_grad.transpose(1, 0, 2),
        w_out_grad.transpose(1, 0, 2),
    )


def solution(mesh):
    tokens = P(("dp", "expert"), None)
    split = P("dp", "expert", None)
    return jax.shard_map(
        on_device,
        mesh=mesh,
        in_specs=(tokens, tokens, split, split, split, split, split),
        out_specs=(tokens, split, split, split),
        check_vma=False,
    )
```

```python
import functools
import jax
import jax.numpy as jnp
from jax import lax
from jax.experimental import pallas as pl
from jax.experimental.pallas import tpu as pltpu
from jax.sharding import PartitionSpec as P

gelu_coef = 0.7978845608028654
cubic_coef = 0.044715
bf16 = jnp.bfloat16
f32 = jnp.float32
i32 = jnp.int32
VMEM_BYTES = 67043328


def gelu_parts(value):
    inner = gelu_coef * (value + cubic_coef * value * value * value)
    tangent = jnp.tanh(inner)
    result = 0.5 * value * (1.0 + tangent)
    slope = 0.5 * (1.0 + tangent) + 0.5 * value * (1.0 - tangent * tangent) * gelu_coef * (
        1.0 + 3.0 * cubic_coef * value * value
    )
    return (result, slope)


def dot(a, b, ca, cb):
    return lax.dot_general(a, b, (((ca,), (cb,)), ((), ())), preferred_element_type=f32)


def loop(count, body):
    def step(i, carry):
        body(i)
        return carry

    lax.fori_loop(0, count, step, 0)


def layer_kernel(
    n_peers, n_ring, slots, group, tile,
    x_ref, g_ref, wi_ref, wo_ref, table_ref, slot_col, gate_col,
    tok_ref, gate_ref, wig_ref, wog_ref,
    full, send_x, send_g, recv_x, recv_g, recv_b, sel, want, pick,
    picked_x, picked_g, scaled, hidden, slope, pre_grad, in_grad, ring,
    ag_send, ag_recv, rs_send, rs_recv, t_send, t_recv, a_send, a_recv, own_sem,
):
    me = lax.axis_index("expert")
    z = lax.axis_index("dp")
    tokens, width = x_ref.shape
    shard = wi_ref.shape[1]
    picks = slot_col.shape[0]
    cap = picks // 2
    n_slots = n_peers * slots
    span = group * slots
    half = n_ring // 2
    tiles = picks // tile
    per_expert = cap // tile

    def rows_of(i):
        return pl.ds(pl.multiple_of(i * tile, tile), tile)

    def expert_rows(e):
        return pl.ds(pl.multiple_of(e * cap, cap), cap)

    def peer_rows(p):
        return pl.ds(pl.multiple_of(p * slots, slots), slots)

    def shard_rows(s):
        return pl.ds(pl.multiple_of(s * shard, shard), shard)

    barrier = pltpu.get_barrier_semaphore()

    def greet(i):
        pl.semaphore_signal(
            barrier, inc=1, device_id={"expert": lax.rem(me + i + 1, n_peers)},
            device_id_type=pl.DeviceIdType.MESH,
        )

    loop(n_peers - 1, greet)
    for step in (1, n_ring - 1):
        pl.semaphore_signal(
            barrier, inc=1, device_id={"dp": lax.rem(z + step, n_ring)},
            device_id_type=pl.DeviceIdType.MESH,
        )
    pl.semaphore_wait(barrier, n_peers + 1)

    def neighbour(d):
        return lax.rem(z + 1 + d * (n_ring - 2), n_ring)

    def ag_copy(m, e, d, s, own):
        holder = lax.rem(z + n_ring - s + d * (2 * s), n_ring)
        place = full.at[m, e, shard_rows(holder), :]
        source = (wi_ref, wo_ref)[m].at[e] if own else place
        return pltpu.make_async_remote_copy(
            src_ref=source, dst_ref=place,
            send_sem=ag_send.at[m, e, d, s], recv_sem=ag_recv.at[m, e, d, s],
            device_id={"dp": neighbour(d)}, device_id_type=pl.DeviceIdType.MESH,
        )

    def ag_step(m, s):
        def one(j):
            e, d = j // 2, j % 2
            if s > 0:
                ag_copy(m, e, d, s - 1, False).wait_recv()
            if s < half:
                ag_copy(m, e, d, s, s == 0).start()

        def last(j):
            if s > 0:
                ag_copy(m, j, j, s - 1, False).wait_recv()
            if s < half:
                ag_copy(m, j, j, s, s == 0).start()

        def tail(e):
            ag_copy(m, e, 1 - e, s - 1, False).wait_recv()

        if s < half - 1:
            loop(4, one)
        else:
            loop(2, last)
            if s == half - 1 and s > 0:
                loop(2, tail)

    def own_copy(m, e):
        return pltpu.make_async_copy(
            (wi_ref, wo_ref)[m].at[e], full.at[m, e, shard_rows(z), :], own_sem.at[m, e]
        )

    ag_step(0, 0)
    ag_step(1, 0)

    def table_copy(q):
        return pltpu.make_async_remote_copy(
            src_ref=table_ref.at[q], dst_ref=want.at[me],
            send_sem=t_send.at[q], recv_sem=t_recv.at[me],
            device_id={"expert": q}, device_id_type=pl.DeviceIdType.MESH,
        )

    def table_arrival(p):
        return pltpu.make_async_remote_copy(
            src_ref=table_ref.at[p], dst_ref=want.at[p],
            send_sem=t_send.at[p], recv_sem=t_recv.at[p],
            device_id={"expert": p}, device_id_type=pl.DeviceIdType.MESH,
        )

    def other(i):
        return lax.rem(me + lax.rem((i + 1) * 13, n_peers), n_peers)

    loop(n_peers - 1, lambda i: table_copy(other(i)).start())
    for m in range(2):
        for e in range(2):
            own_copy(m, e).start()
    mine = pltpu.make_async_copy(table_ref.at[me], want.at[me], own_sem.at[2, 0])
    mine.start()
    mine.wait()
    loop(n_peers - 1, lambda i: table_arrival(other(i)).wait_recv())

    for k in range(n_peers // group):
        asked = jnp.sum(want[k * group : (k + 1) * group], axis=0)
        token = lax.broadcasted_iota(i32, (tokens, span), 0) + 1
        sel[:, k * span : (k + 1) * span] = jnp.where(token == asked, 1.0, 0.0).astype(bf16)

    def gather(source, target):
        for k in range(n_peers // group):
            rows = slice(k * span, (k + 1) * span)
            target[rows, :] = dot(sel[:, rows], source[...], 0, 0).astype(bf16)

    def row_copy(phase, source, target, q):
        return pltpu.make_async_remote_copy(
            src_ref=source.at[peer_rows(q), :], dst_ref=target.at[peer_rows(me), :],
            send_sem=a_send.at[phase, q], recv_sem=a_recv.at[phase, me],
            device_id={"expert": q}, device_id_type=pl.DeviceIdType.MESH,
        )

    def row_arrival(phase, source, target, p):
        return pltpu.make_async_remote_copy(
            src_ref=source.at[peer_rows(p), :], dst_ref=target.at[peer_rows(p), :],
            send_sem=a_send.at[phase, p], recv_sem=a_recv.at[phase, p],
            device_id={"expert": p}, device_id_type=pl.DeviceIdType.MESH,
        )

    def own_rows(phase, source, target):
        return pltpu.make_async_copy(
            source.at[peer_rows(me), :], target.at[peer_rows(me), :], own_sem.at[3, phase]
        )

    def send_all(phase, source, target):
        loop(n_peers - 1, lambda i: row_copy(phase, source, target, other(i)).start())
        own_rows(phase, source, target).start()

    def receive_all(phase, source, target):
        own_rows(phase, source, target).wait()
        loop(n_peers - 1, lambda i: row_arrival(phase, source, target, other(i)).wait_recv())

    def sent_all(phase, source, target):
        loop(n_peers - 1, lambda i: row_copy(phase, source, target, other(i)).wait_send())

    gather(x_ref, send_x)
    send_all(0, send_x, recv_x)
    if half > 1:
        ag_step(0, 1)
    gather(g_ref, send_g)
    send_all(1, send_g, recv_g)

    def make_pick(i):
        at = lax.broadcasted_iota(i32, (tile, n_slots), 1)
        pick[rows_of(i), :] = jnp.where(slot_col[rows_of(i), :] == at, 1.0, 0.0).astype(bf16)

    loop(tiles, make_pick)
    for s in range(2, half):
        ag_step(0, s)
    if half > 1:
        ag_step(1, 1)
    ag_step(0, half)
    for e in range(2):
        own_copy(0, e).wait()
    receive_all(0, send_x, recv_x)

    def forward(i):
        rows = rows_of(i)
        picked = dot(pick[rows, :], recv_x[...], 1, 0).astype(bf16)
        picked_x[rows, :] = picked
        value, grade = gelu_parts(dot(picked, full[0, i // per_expert], 1, 0))
        hidden[rows, :] = value.astype(bf16)
        slope[rows, :] = grade

    loop(per_expert, forward)
    if half > 2:
        ag_step(1, 2)
    loop(per_expert, lambda i: forward(i + per_expert))
    for s in range(3, half):
        ag_step(1, s)
    receive_all(1, send_g, recv_g)

    def arrive_grad(i):
        rows = rows_of(i)
        grad = dot(pick[rows, :], recv_g[...], 1, 0).astype(bf16)
        picked_g[rows, :] = grad
        scaled[rows, :] = (gate_col[rows, :] * grad.astype(f32)).astype(bf16)

    def part(m, e, t):
        columns = pl.ds(pl.multiple_of(t * shard, shard), shard)
        left, right = ((picked_x, pre_grad), (hidden, scaled))[m]
        return dot(left[expert_rows(e), columns], right[expert_rows(e), :], 0, 0)

    def rs_copy(m, e, d, s):
        return pltpu.make_async_remote_copy(
            src_ref=ring.at[m, e, d, s], dst_ref=ring.at[m, e, d, s + 1],
            send_sem=rs_send.at[m, e, d, s], recv_sem=rs_recv.at[m, e, d, s],
            device_id={"dp": neighbour(d)}, device_id_type=pl.DeviceIdType.MESH,
        )

    def rs_hop(m, e, d, s, hops):
        far = hops - s
        block = part(m, e, lax.rem(z + n_ring + far - 2 * d * far, n_ring))
        if s > 0:
            rs_copy(m, e, d, s - 1).wait_recv()
            block = block + ring[m, e, d, s].astype(f32)
        ring[m, e, d, s] = block.astype(bf16)
        rs_copy(m, e, d, s).start()

    def rs_first(m, e):
        rs_hop(m, e, e, 0, half)
        if half > 1:
            rs_hop(m, e, 1 - e, 0, half - 1)

    def rs_step(m, s):
        loop(2, lambda e: rs_hop(m, e, e, s, half))
        if s < half - 1:
            loop(2, lambda e: rs_hop(m, e, 1 - e, s, half - 1))

    def rs_final(m, target):
        def one(e):
            total = part(m, e, z)
            rs_copy(m, e, e, half - 1).wait_recv()
            total = total + ring[m, e, e, half].astype(f32)
            if half > 1:
                rs_copy(m, e, 1 - e, half - 2).wait_recv()
                total = total + ring[m, e, 1 - e, half - 1].astype(f32)
            target[e] = total.astype(bf16)

        loop(2, one)

    def backward(i):
        rows = rows_of(i)
        wide = dot(scaled[rows, :], full[1, i // per_expert], 1, 1)
        pre_grad[rows, :] = (wide * slope[rows, :]).astype(bf16)

    def to_input(i):
        rows = rows_of(i)
        in_grad[rows, :] = dot(pre_grad[rows, :], full[0, i // per_expert], 1, 1).astype(bf16)

    def back(k):
        rows = pl.ds(pl.multiple_of(k * span, span), span)
        send_x[rows, :] = dot(pick[:, rows], in_grad[...], 0, 0).astype(bf16)

    def gate_part(i):
        rows = rows_of(i)
        wide = dot(hidden[rows, :], full[1, i // per_expert], 1, 0)
        gate_ref[rows, :] = jnp.sum(picked_g[rows, :].astype(f32) * wide, axis=1, keepdims=True)

    def grads_of(e):
        loop(per_expert, lambda i: arrive_grad(i + e * per_expert))
        rs_first(1, e)

    def back_of(e):
        loop(per_expert, lambda i: backward(i + e * per_expert))
        rs_first(0, e)

    loop(2, grads_of)
    ag_step(1, half)
    for e in range(2):
        own_copy(1, e).wait()
    loop(2, back_of)
    loop(tiles, to_input)
    if half > 1:
        rs_step(1, 1)
    sent_all(0, send_x, recv_x)
    loop(n_peers // group, back)
    send_all(2, send_x, recv_b)
    if half > 1:
        rs_step(0, 1)
    loop(tiles, gate_part)
    for s in range(2, half):
        rs_step(1, s)
        rs_step(0, s)
    receive_all(2, send_x, recv_b)
    tok_ref[...] = dot(sel[...], recv_b[...], 1, 0).astype(bf16)
    rs_final(1, wog_ref)
    rs_final(0, wig_ref)

    loop(n_peers - 1, lambda i: table_copy(other(i)).wait_send())
    sent_all(1, send_g, recv_g)
    sent_all(2, send_x, recv_b)
    for m in range(2):
        for s in range(half):
            for e in range(2):
                for d in range(2):
                    if s < half - 1 or e == d:
                        ag_copy(m, e, d, s, s == 0).wait_send()
                        rs_copy(m, e, d, s).wait_send()


def on_device(activations, out_grad, w_in, w_out, token_lists, valid_mask, gate_weights):
    n_peers = lax.axis_size("expert")
    n_ring = lax.axis_size("dp")
    me = lax.axis_index("expert")
    tok_local, width = activations.shape
    _, exp_local, cap_len = token_lists.shape
    shard, _, hid = w_in.shape
    picks = exp_local * cap_len
    slots = max(2, 3 * picks // (2 * n_peers))
    n_slots = n_peers * slots
    group = min(8, n_peers)
    tile = min(256, cap_len)

    flat = token_lists.reshape(picks)
    live = valid_mask.reshape(picks) == 1
    owners = jnp.where(live, flat // tok_local, -1)
    local = flat % tok_local
    peers = jnp.arange(n_peers, dtype=i32)
    hits = (owners[:, None] == peers[None, :]).astype(bf16)
    order = jnp.arange(picks, dtype=i32)
    earlier = (order[None, :] < order[:, None]).astype(bf16)
    rank_all = dot(earlier, hits, 1, 0)
    before = jnp.sum(rank_all * hits.astype(f32), axis=1).astype(i32)
    slot_of = jnp.where(live, owners * slots + before, -1)
    lane = before + (me % group) * slots
    place = (lane[:, None] == jnp.arange(group * slots, dtype=i32)[None, :]).astype(bf16)
    high = (local // 32).astype(bf16)[:, None]
    low = (local % 32 + 1).astype(bf16)[:, None]
    both = jnp.concatenate([hits * high, hits * low], axis=1)
    coded = dot(both, place, 0, 0).astype(i32)
    table = coded[:n_peers] * 32 + coded[n_peers:]
    gates = (gate_weights * valid_mask.astype(f32)).reshape(picks, 1)

    vmem = pl.BlockSpec(memory_space=pltpu.VMEM)
    dma = pltpu.SemaphoreType.DMA
    rows = (n_slots, width)
    half = n_ring // 2
    token_grad, gate_grad, w_in_grad, w_out_grad = pl.pallas_call(
        functools.partial(layer_kernel, n_peers, n_ring, slots, group, tile),
        out_shape=(
            jax.ShapeDtypeStruct((tok_local, width), bf16),
            jax.ShapeDtypeStruct((picks, 1), f32),
            jax.ShapeDtypeStruct((exp_local, shard, hid), bf16),
            jax.ShapeDtypeStruct((exp_local, shard, width), bf16),
        ),
        in_specs=[vmem] * 7,
        out_specs=(vmem,) * 4,
        scratch_shapes=[
            pltpu.VMEM((2, exp_local, width, hid), bf16),
            pltpu.VMEM(rows, bf16),
            pltpu.VMEM(rows, bf16),
            pltpu.VMEM(rows, bf16),
            pltpu.VMEM(rows, bf16),
            pltpu.VMEM(rows, bf16),
            pltpu.VMEM((tok_local, n_slots), bf16),
            pltpu.VMEM((n_peers, 1, group * slots), i32),
            pltpu.VMEM((picks, n_slots), bf16),
            pltpu.VMEM((picks, width), bf16),
            pltpu.VMEM((picks, width), bf16),
            pltpu.VMEM((picks, width), bf16),
            pltpu.VMEM((picks, hid), bf16),
            pltpu.VMEM((picks, hid), f32),
            pltpu.VMEM((picks, hid), bf16),
            pltpu.VMEM((picks, width), bf16),
            pltpu.VMEM((2, exp_local, 2, half + 1, shard, width), bf16),
            dma((2, 2, 2, half)),
            dma((2, 2, 2, half)),
            dma((2, 2, 2, half)),
            dma((2, 2, 2, half)),
            dma((n_peers,)),
            dma((n_peers,)),
            dma((3, n_peers)),
            dma((3, n_peers)),
            dma((4, 3)),
        ],
        compiler_params=pltpu.CompilerParams(
            collective_id=0, has_side_effects=True, vmem_limit_bytes=VMEM_BYTES
        ),
    )(
        activations,
        out_grad,
        w_in.transpose(1, 0, 2),
        w_out.transpose(1, 0, 2),
        table.reshape(n_peers, 1, group * slots),
        slot_of.reshape(picks, 1),
        gates,
    )
    return (
        token_grad,
        gate_grad.reshape(1, exp_local, cap_len),
        w_in_grad.transpose(1, 0, 2),
        w_out_grad.transpose(1, 0, 2),
    )


def solution(mesh):
    tokens = P(("dp", "expert"), None)
    split = P("dp", "expert", None)
    return jax.shard_map(
        on_device,
        mesh=mesh,
        in_specs=(tokens, tokens, split, split, split, split, split),
        out_specs=(tokens, split, split, split),
        check_vma=False,
    )
```
